32 devices in a mesh: dp: 8 (over y, x, core), pipe: 4 (over z).
Axes of the slice: x: 2, y: 2, z: 4, core: 2. Of those that a mesh axis runs over, the one named last changes fastest.
Arguments:
- shallow: bfloat16 [2048, 8192], P('dp'), may hold values from -8 to 8
- teacher: bfloat16 [2048, 8192], P(('dp', 'pipe')), may hold values from -8 to 8
- positions: int32 [2048], P('dp'), may hold values from 0 to 4095
- segments: int32 [2048], P('dp'), may hold values from 0 to 127, never falling along the last dimension, each value on 1 to 64 neighbouring positions
- in_gain: float32 [8192], replicated, may hold values from 0.2 to 4.5
- w_query: bfloat16 [8192, 4096], P('dp', 'pipe'), may hold values from -0.0625 to 0.0625
- w_keyval: bfloat16 [8192, 1024], P('dp', 'pipe'), may hold values from -0.0625 to 0.0625
- w_output: bfloat16 [4096, 8192], P('pipe', 'dp'), may hold values from -0.09375 to 0.09375
Outputs:
- loss: float32 [], replicated
- step_query: float32 [8192, 4096], P('dp', 'pipe')
- step_keyval: float32 [8192, 1024], P('dp', 'pipe')
- step_output: float32 [4096, 8192], P('pipe', 'dp')
The draws below stay inside these ranges and needn't reach their ends.
Inputs may be any that keep to these rules, and one draw needn't show every extreme that they name: `segments`: ids never fall along the rows; every segment covers 1 to 64 rows.
All inputs are finite; a program needn't handle non-finite values.
Results may differ from the reference program's by a relative error of at most 0.023.
Values may be sent and summed in bfloat16 or wider, within the bound.
No kernel may reach another device: no remote copies, remote signals or barrier semaphores. Data moves between devices by JAX's collectives and lax.ppermute only.
A program may use at most 128 MiB of HBM per device.

```python
import math
import jax
import jax.numpy as jnp
import numpy as np
from jax import lax

D = 8192
HD = 128
QH = 32
KV = 4
R = 256
ROWS = 2048
N_DP = 8
N_PIPE = 4


def shared_rows(key):
    base = jax.random.fold_in(key, 7301)
    raw = jnp.clip(jax.random.normal(base, (ROWS, D), jnp.float32), -6.0, 6.0)
    return raw


def draw_shallow(key, part):
    return jnp.clip(shared_rows(key), -8.0, 8.0).astype(jnp.bfloat16)


def draw_teacher(key, part):
    source = jnp.clip(shared_rows(key), -8.0, 8.0)
    groups = ROWS // R
    block_rows = R // N_PIPE
    rolled = jnp.roll(source.reshape(groups, N_PIPE, block_rows, D), -1, axis=1).reshape(ROWS, D)
    order = jnp.arange(ROWS).astype(jnp.float32).reshape(groups, N_PIPE, block_rows)
    target_index = jnp.roll(order, -1, axis=1).reshape(ROWS, 1)
    fraction = target_index / ROWS
    noise_key = jax.random.fold_in(key, 7302)
    weight = 0.9 * (1.0 - fraction)
    noise = jnp.clip(jax.random.normal(noise_key, (ROWS, D), jnp.float32), -6.0, 6.0)
    mixed = weight * rolled + jnp.sqrt(1.0 - weight * weight) * noise
    return jnp.clip(mixed, -8.0, 8.0).astype(jnp.bfloat16)


def draw_in_gain(key, part):
    steps = jnp.arange(D).astype(jnp.float32) / (D - 1)
    trend = jnp.exp(jnp.log(0.5) + steps * (jnp.log(2.0) - jnp.log(0.5)))
    rough = jax.random.uniform(jax.random.fold_in(key, 7311), (D,), jnp.float32, 0.8, 1.25)
    return jnp.clip(trend * rough, 0.2, 4.5)


def touch_ends(values, own_key, smallest, largest):
    place = [jax.random.randint(jax.random.fold_in(own_key, axis), (), 0, length) for axis, length in enumerate(values.shape)]
    widest = values.shape.index(max(values.shape))
    next_to = place[:widest] + [(place[widest] + 1) % values.shape[widest]] + place[widest + 1:]
    return values.at[tuple(place)].set(smallest).at[tuple(next_to)].set(largest)


def levels(own_key, dims, split, least, top_value):
    def one(axis_at, blocks):
        heights = jax.random.uniform(jax.random.fold_in(jax.random.fold_in(own_key, 6), axis_at), (blocks,), jnp.float32, least / len(split), top_value / len(split))
        return jnp.repeat(jnp.exp(heights), dims[axis_at] // blocks).reshape((-1,) + (1,) * (len(dims) - axis_at - 1))

    loudness = one(*split[0])
    for cut in split[1:]:
        loudness = loudness * one(*cut)
    return loudness


def length_profile(number_of, total, reach, lean):
    loads = [(1 << 20) // math.isqrt(rank ** lean) + 1 for rank in range(2, number_of + 1)]
    rest, holding = total - reach - (number_of - 1), [1] * (number_of - 1)
    while rest > 0:
        candidates = [i for i in range(number_of - 1) if holding[i] < reach]
        mass, budget = sum([loads[i] for i in candidates]), rest
        for i in candidates:
            addition = min(reach - holding[i], max(1, budget * loads[i] // mass), rest)
            holding[i] = holding[i] + addition
            rest = rest - addition
    return np.array([reach] + holding)


def uneven(key, number_of, total, reach, lean):
    if number_of == 2:
        one = jax.random.randint(key, (), max(1, total - reach), min(reach, total - 1) + 1)
        return jnp.stack([one, total - one])
    sizes = jnp.asarray(length_profile(number_of, total, reach, lean), jnp.int32)
    twos = (number_of - 1) // 2
    giver, sink = sizes[1:1 + 2 * twos:2], sizes[2:2 + 2 * twos:2]
    slack = jnp.minimum(giver - 1, reach - sink)
    moved = jax.random.randint(jax.random.fold_in(key, 1), (twos,), 0, 1 << 20) % (slack + 1)
    sizes = sizes.at[1:1 + 2 * twos:2].set(giver - moved).at[2:2 + 2 * twos:2].set(sink + moved)
    return sizes[jax.random.permutation(jax.random.fold_in(key, 2), number_of)]


def bell_draw(rng, extent, deviation, limit, split=(), dtype=jnp.bfloat16):
    array = jax.random.normal(rng, extent, jnp.float32) * deviation
    if len(split) > 0:
        array = levels(rng, extent, split, -0.22, 0.18) * array
    return jnp.clip(array, min=-limit, max=limit).astype(dtype)


def setup_inputs(seed: int = 0) -> dict:
    seeds = jax.random.split(jax.random.key(seed), 9)
    return {
        "shallow": draw_shallow(jax.random.fold_in(seeds[8], 71), 0),
        "teacher": draw_teacher(jax.random.fold_in(seeds[8], 71), 0),
        "positions": touch_ends(jax.random.randint(seeds[2], (ROWS,), 0, 4096), jax.random.fold_in(seeds[2], 1), 0, 4095).astype(jnp.int32),
        "segments": jnp.searchsorted(jnp.cumsum(uneven(seeds[3], ROWS // 16, ROWS, 64, 0)), jnp.arange(ROWS), side="right").astype(jnp.int32),
        "in_gain": draw_in_gain(jax.random.fold_in(seeds[8], 71), 0),
        "w_query": bell_draw(seeds[5], (D, QH * HD), D ** -0.5, 0.0625, ((0, 8), (1, 4))),
        "w_keyval": bell_draw(seeds[6], (D, 2 * KV * HD), D ** -0.5, 0.0625, ((0, 8), (1, 4))),
        "w_output": bell_draw(seeds[7], (QH * HD, D), (QH * HD) ** -0.5, 0.09375, ((0, 4), (1, 8))),
    }


theta_base = 10000.0
norm_eps = 1e-05
cosine_eps = 1e-06
mean_eps = 1e-12
mask_fill = -1e+30

def normalize_rows(rows_in, in_gain):
    widened = rows_in.astype(jnp.float32)
    spread = lax.optimization_barrier(jnp.mean(widened * widened, axis=-1, keepdims=True))
    return (widened * lax.rsqrt(spread + norm_eps) * in_gain[None, :]).astype(jnp.bfloat16)

def rotary_tables(positions, head_width):
    half_width = head_width // 2
    exponent = jnp.arange(half_width).astype(jnp.float32) * (2.0 / head_width)
    inverse = jnp.power(jnp.float32(theta_base), -exponent)
    angle_table = positions.astype(jnp.float32)[:, None] * inverse[None, :]
    return (jnp.cos(angle_table), jnp.sin(angle_table))

def rotate(values, cosine, sine_table):
    half_width = values.shape[-1] // 2
    leading = values[..., :half_width]
    trailing = values[..., half_width:]
    cosine_row = cosine[:, None, :]
    sine_row = sine_table[:, None, :]
    return jnp.concatenate([leading * cosine_row - trailing * sine_row, trailing * cosine_row + leading * sine_row], axis=-1)

def unrotate(values, cosine, sine_table):
    half_width = values.shape[-1] // 2
    leading = values[..., :half_width]
    trailing = values[..., half_width:]
    cosine_row = cosine[:, None, :]
    sine_row = sine_table[:, None, :]
    return jnp.concatenate([leading * cosine_row + trailing * sine_row, trailing * cosine_row - leading * sine_row], axis=-1)

def attend(queries, keys_head, values_head, allowed):
    score_scale = 1.0 / math.sqrt(queries.shape[-1])
    scores = jnp.einsum('rhd,khd->hrk', queries.astype(jnp.float32), keys_head.astype(jnp.float32)) * score_scale
    scores = jnp.where(allowed[None], scores, mask_fill)
    highest = lax.optimization_barrier(jnp.max(scores, axis=-1, keepdims=True))
    weights = jnp.exp(scores - highest)
    softmax_rows = weights / lax.optimization_barrier(jnp.sum(weights, axis=-1, keepdims=True))
    softmax_low = softmax_rows.astype(jnp.bfloat16)
    attended = jnp.einsum('hrk,khd->rhd', softmax_low.astype(jnp.float32), values_head.astype(jnp.float32)).astype(jnp.bfloat16)
    return (softmax_rows, softmax_low, attended)

def attend_grad(softmax_rows, softmax_low, queries, keys_head, values_head, att_grad):
    score_scale = 1.0 / math.sqrt(queries.shape[-1])
    inner_prod = jnp.einsum('rhd,khd->hrk', att_grad.astype(jnp.float32), values_head.astype(jnp.float32))
    centred = inner_prod - lax.optimization_barrier(jnp.sum(softmax_rows * inner_prod, axis=-1, keepdims=True))
    score_grad = (softmax_rows * centred * score_scale).astype(jnp.bfloat16)
    query_part = jnp.einsum('hrk,khd->rhd', score_grad.astype(jnp.float32), keys_head.astype(jnp.float32))
    key_part = jnp.einsum('hrk,rhd->khd', score_grad.astype(jnp.float32), queries.astype(jnp.float32))
    value_part = jnp.einsum('hrk,rhd->khd', softmax_low.astype(jnp.float32), att_grad.astype(jnp.float32))
    return (query_part, key_part, value_part)

def held_low(values):
    return lax.optimization_barrier(values.astype(jnp.bfloat16)).astype(jnp.float32)

def contract_rows(left, right):
    return lax.dot_general(left, right, (((0,), (0,)), ((), ())), preferred_element_type=jnp.float32)

def reference(shallow, teacher, positions, segments, in_gain, w_query, w_keyval, w_output):
    block_rows = R // N_PIPE
    head_group = QH // KV
    group_cols = QH * HD // N_PIPE
    shallow_groups = shallow.reshape(N_DP, R, D)
    teacher_groups = jnp.roll(teacher.reshape(N_DP, N_PIPE, block_rows, D), 1, axis=1).reshape(N_DP, R, D)
    position_groups = positions.reshape(N_DP, R)
    segment_groups = segments.reshape(N_DP, R)
    row_order = jnp.arange(R)

    def one_group(running, inputs):
        grad_query, grad_keyval, grad_output, loss_sum = running
        shallow_rows, target_rows, position_rows, segment_rows = inputs
        normed = normalize_rows(shallow_rows, in_gain)
        cosine, sine_table = rotary_tables(position_rows, HD)
        query_proj = jnp.dot(normed, w_query, preferred_element_type=jnp.float32).reshape(R, QH, HD)
        queries = rotate(query_proj, cosine, sine_table).astype(jnp.bfloat16)
        keyval_proj = jnp.dot(normed, w_keyval, preferred_element_type=jnp.float32).reshape(R, KV, 2, HD)
        keys = rotate(keyval_proj[:, :, 0], cosine, sine_table).astype(jnp.bfloat16)
        values = keyval_proj[:, :, 1].astype(jnp.bfloat16)
        keys_head = jnp.tile(keys, (1, head_group, 1))
        values_head = jnp.tile(values, (1, head_group, 1))
        allowed = (segment_rows[:, None] == segment_rows[None, :]) & (row_order[None, :] <= row_order[:, None])
        softmax_rows, softmax_low, attended = attend(queries, keys_head, values_head, allowed)
        att_flat = attended.reshape(R, QH * HD)
        head_sum = jnp.zeros((R, D), jnp.float32)
        for block_index in range(N_PIPE):
            low_col = block_index * group_cols
            head_sum = head_sum + held_low(jnp.dot(att_flat[:, low_col:low_col + group_cols], w_output[low_col:low_col + group_cols], preferred_element_type=jnp.float32))
        output = shallow_rows.astype(jnp.float32) + head_sum
        target = target_rows.astype(jnp.float32)
        norm_out = jnp.sqrt(lax.optimization_barrier(jnp.sum(output * output, axis=-1, keepdims=True)) + cosine_eps)
        norm_tar = jnp.sqrt(lax.optimization_barrier(jnp.sum(target * target, axis=-1, keepdims=True)) + cosine_eps)
        cosine_sim = lax.optimization_barrier(jnp.sum(output * target, axis=-1, keepdims=True)) / (norm_out * norm_tar)
        loss_part = jnp.sum(1.0 - cosine_sim)
        out_grad = (-(target / (norm_out * norm_tar) - cosine_sim * output / (norm_out * norm_out)) / ROWS).astype(jnp.bfloat16)
        att_grad = lax.dot_general(out_grad, w_output, (((1,), (1,)), ((), ())), preferred_element_type=jnp.float32).astype(jnp.bfloat16).reshape(R, QH, HD)
        query_part, key_part, value_part = attend_grad(softmax_rows, softmax_low, queries, keys_head, values_head, att_grad)
        query_grad = unrotate(query_part, cosine, sine_table).astype(jnp.bfloat16).reshape(R, QH * HD)
        key_sum = lax.optimization_barrier(jnp.sum(key_part.reshape(R, head_group, KV, HD), axis=1))
        value_sum = lax.optimization_barrier(jnp.sum(value_part.reshape(R, head_group, KV, HD), axis=1))
        keyval_grad = jnp.stack([unrotate(key_sum, cosine, sine_table), value_sum], axis=2).astype(jnp.bfloat16).reshape(R, 2 * KV * HD)
        grad_query = grad_query + held_low(contract_rows(normed, query_grad))
        grad_keyval = grad_keyval + held_low(contract_rows(normed, keyval_grad))
        grad_output = grad_output + held_low(contract_rows(att_flat, out_grad))
        return ((grad_query, grad_keyval, grad_output, loss_sum + loss_part), None)
    start_state = (jnp.zeros((D, QH * HD), jnp.float32), jnp.zeros((D, 2 * KV * HD), jnp.float32), jnp.zeros((QH * HD, D), jnp.float32), jnp.zeros((), jnp.float32))
    final_state, _ = lax.scan(one_group, start_state, (shallow_groups, teacher_groups, position_groups, segment_groups))
    grad_query, grad_keyval, grad_output, loss_sum = final_state
    square_total = jnp.sum(grad_query * grad_query) + jnp.sum(grad_keyval * grad_keyval) + jnp.sum(grad_output * grad_output)
    grad_rms = jnp.sqrt(square_total / (D * (2 * QH * HD + 2 * KV * HD)) + mean_eps)
    return (loss_sum / ROWS, grad_query / grad_rms, grad_keyval / grad_rms, grad_output / grad_rms)
```

```python
import math

import jax
import jax.numpy as jnp
from jax import lax
from jax.sharding import PartitionSpec as P

D = 8192
HD = 128
QH = 32
KV = 4


theta_base = 10000.0
norm_eps = 1e-05
cosine_eps = 1e-06
mean_eps = 1e-12
mask_fill = -1e30


def rotary_tables(positions, head_width):
    half_width = head_width // 2
    exponent = jnp.arange(half_width).astype(jnp.float32) * (2.0 / head_width)
    inverse = jnp.power(jnp.float32(theta_base), -exponent)
    angle_table = positions.astype(jnp.float32)[:, None] * inverse[None, :]
    return (jnp.cos(angle_table), jnp.sin(angle_table))


def rotate(values, cosine, sine_table):
    half_width = values.shape[-1] // 2
    leading = values[..., :half_width]
    trailing = values[..., half_width:]
    cosine_row = cosine[:, None, :]
    sine_row = sine_table[:, None, :]
    return jnp.concatenate(
        [leading * cosine_row - trailing * sine_row, trailing * cosine_row + leading * sine_row],
        axis=-1,
    )


def unrotate(values, cosine, sine_table):
    half_width = values.shape[-1] // 2
    leading = values[..., :half_width]
    trailing = values[..., half_width:]
    cosine_row = cosine[:, None, :]
    sine_row = sine_table[:, None, :]
    return jnp.concatenate(
        [leading * cosine_row + trailing * sine_row, trailing * cosine_row - leading * sine_row],
        axis=-1,
    )


def by_bit(value, bit, axis):
    count = lax.axis_size(axis)
    return lax.ppermute(value, axis, [(source, source ^ bit) for source in range(count)])


def by_shift(value, steps, axis):
    count = lax.axis_size(axis)
    pairs = [(source, (source + steps) % count) for source in range(count)]
    return lax.ppermute(value, axis, pairs)


def bits_of(axis):
    count = lax.axis_size(axis)
    bits = [1 << level for level in range(count.bit_length() - 1)]
    assert bits and 2 * bits[-1] == count
    return bits


def peer_order(axis):
    order = [0]
    for bit in bits_of(axis)[1:]:
        order = order + [peer | bit for peer in order]
    return order + [peer | 1 for peer in order]


def exchange_slices(rows_in, axis):
    count = lax.axis_size(axis)
    width = rows_in.shape[1] // count
    rank = lax.axis_index(axis)
    found = {}
    for peer in reversed(range(count)):
        piece = lax.dynamic_slice_in_dim(rows_in, (rank ^ peer) * width, width, 1)
        found[peer] = by_bit(piece, peer, axis) if peer else piece
    return found


def reduce_peers(keep, send, axis):
    low = jnp.bfloat16
    bits = bits_of(axis)
    total = keep.astype(jnp.float32) + by_bit(send.astype(low), 1, axis).astype(jnp.float32)
    far = bits[1:]
    if not far:
        return total[0]
    half = total.shape[1] // 2
    done = []
    for part, order in ((total[:, :half], far[::-1]), (total[:, half:], far)):
        cube = part.reshape((2,) * len(far) + part.shape[1:])
        left = list(far[::-1])
        for bit in order:
            at = left.index(bit)
            left.pop(at)
            going = lax.index_in_dim(cube, 1, at, False).astype(low)
            cube = lax.index_in_dim(cube, 0, at, False) + by_bit(going, bit, axis).astype(jnp.float32)
        done.append(cube)
    return jnp.concatenate(done, axis=0)


def gather_peers(value, axis):
    bits = bits_of(axis)
    found = {0: value}
    if len(bits) == 3:
        core, near, far = bits
        half = value.shape[0] // 2
        found[near] = by_bit(value, near, axis)
        found[far] = by_bit(value, far, axis)
        found[core] = by_bit(value, core, axis)
        first = by_bit(found[far][:half], near, axis)
        second = by_bit(found[near][half:], far, axis)
        found[near | core] = by_bit(found[near], core, axis)
        found[far | core] = by_bit(found[far], core, axis)
        found[near | far] = jnp.concatenate([first, second], axis=0)
        found[near | far | core] = jnp.concatenate(
            [by_bit(first, core, axis), by_bit(second, core, axis)], axis=0
        )
        return found
    for bit in bits[1:] + bits[:1]:
        found.update({peer | bit: by_bit(piece, bit, axis) for peer, piece in list(found.items())})
    return found


def gather_line(value, axis):
    count = lax.axis_size(axis)
    up = [(source, source + 1) for source in range(count - 1)]
    down = [(source + 1, source) for source in range(count - 1)]
    below, above = [value], [value]
    for _ in range(count - 1):
        below.append(lax.ppermute(below[-1], axis, up))
        above.append(lax.ppermute(above[-1], axis, down))
    return [value] + [above[m] + below[count - m] for m in range(1, count)]


def sum_peers(value, axis):
    for bit in bits_of(axis):
        value = value + by_bit(value, bit, axis)
    return value


def sum_peer_rows(value, axis):
    bits = bits_of(axis)
    slots = [1] + bits[:0:-1]
    shape = value.shape
    for bit in bits:
        cube = value.reshape((2,) * len(bits) + shape[1:])
        moved = by_bit(value, bit, axis).reshape(cube.shape)
        value = (cube + jnp.flip(moved, slots.index(bit))).reshape(shape)
    return value


def attend(queries, keys, values, allowed):
    score_scale = 1.0 / math.sqrt(queries.shape[-1])
    scores = (
        jnp.einsum("rakd,jkd->akrj", queries, keys, preferred_element_type=jnp.float32)
        * score_scale
    )
    scores = jnp.where(allowed[None, None], scores, mask_fill)
    highest = jnp.max(scores, axis=-1, keepdims=True)
    weights = jnp.exp(scores - highest)
    softmax_rows = weights / jnp.sum(weights, axis=-1, keepdims=True)
    softmax_low = softmax_rows.astype(jnp.bfloat16)
    attended = jnp.einsum(
        "akrj,jkd->rakd", softmax_low, values, preferred_element_type=jnp.float32
    ).astype(jnp.bfloat16)
    return (softmax_rows, softmax_low, attended)


def attend_grad(softmax_rows, softmax_low, queries, keys, values, att_grad):
    score_scale = 1.0 / math.sqrt(queries.shape[-1])
    inner_prod = jnp.einsum("rakd,jkd->akrj", att_grad, values, preferred_element_type=jnp.float32)
    centred = inner_prod - jnp.sum(softmax_rows * inner_prod, axis=-1, keepdims=True)
    score_grad = (softmax_rows * centred * score_scale).astype(jnp.bfloat16)
    query_part = jnp.einsum("akrj,jkd->rakd", score_grad, keys, preferred_element_type=jnp.float32)
    key_part = jnp.einsum("akrj,rakd->jkd", score_grad, queries, preferred_element_type=jnp.float32)
    value_part = jnp.einsum(
        "akrj,rakd->jkd", softmax_low, att_grad, preferred_element_type=jnp.float32
    )
    return (query_part, key_part, value_part)


def contract_rows(left, right):
    return lax.dot_general(
        left, right, (((0,), (0,)), ((), ())), preferred_element_type=jnp.float32
    )


def contract_cols(left, right):
    return lax.dot_general(
        left, right, (((1,), (1,)), ((), ())), preferred_element_type=jnp.float32
    )


def per_device(shallow, teacher, positions, segments, in_gain, w_query, w_keyval, w_output):
    low = jnp.bfloat16
    wide = jnp.float32
    group_rows, model_width = shallow.shape
    pipe_count = lax.axis_size("pipe")
    data_count = lax.axis_size("dp")
    pipe_rank = lax.axis_index("pipe")
    data_rank = lax.axis_index("dp")
    block_rows = group_rows // pipe_count
    head_cols = w_query.shape[1]
    local_heads = head_cols // HD
    keyval_cols = w_keyval.shape[1]
    keyval_blocks = keyval_cols // HD
    slice_cols = w_output.shape[1]
    all_rows = group_rows * data_count
    param_count = D * (2 * QH * HD + 2 * KV * HD)
    assert local_heads % KV == 0
    order = peer_order("dp")
    half_count = data_count // 2

    found = exchange_slices(shallow, "dp")
    columns = jnp.concatenate([found[peer] for peer in order], axis=0)
    gain = lax.dynamic_slice_in_dim(in_gain, data_rank * slice_cols, slice_cols, 0)[:, None]
    w_both = (jnp.concatenate([w_query, w_keyval], axis=1).astype(wide) * gain).astype(low)
    both_cols = head_cols + keyval_cols
    split = half_count * group_rows
    send = jnp.dot(columns[split:], w_both, preferred_element_type=wide).astype(low)
    keep = jnp.dot(columns[:split], w_both, preferred_element_type=wide)
    spread = jnp.mean(jnp.square(shallow.astype(wide)), axis=-1, keepdims=True)
    row_scale = lax.rsqrt(spread + norm_eps)
    proj = reduce_peers(
        keep.reshape(half_count, group_rows, both_cols),
        send.reshape(half_count, group_rows, both_cols),
        "dp",
    )
    proj = proj * row_scale

    out_weights = jnp.concatenate(gather_line(w_output, "pipe"), axis=0)
    teacher_found = exchange_slices(teacher, "dp")
    target = jnp.concatenate([teacher_found[peer] for peer in order], axis=0).astype(wide)

    cosine, sine_table = rotary_tables(positions, HD)
    queries = rotate(proj[:, :head_cols].reshape(group_rows, local_heads, HD), cosine, sine_table)
    queries = queries.astype(low).reshape(group_rows, local_heads // KV, KV, HD)
    keyval_local = proj[:, head_cols:].reshape(group_rows, keyval_blocks, HD)
    block_ids = pipe_rank * keyval_blocks + jnp.arange(keyval_blocks)
    is_key = (block_ids % 2 == 0)[None, :, None]
    keyval_local = jnp.where(is_key, rotate(keyval_local, cosine, sine_table), keyval_local)
    keyval_local = keyval_local.astype(low).reshape(group_rows, keyval_cols)
    pieces = [keyval_local] + [by_shift(keyval_local, -m, "pipe") for m in range(1, pipe_count)]
    keyval_all = jnp.roll(jnp.stack(pieces), pipe_rank, axis=0)
    keyval_all = keyval_all.transpose(1, 0, 2).reshape(group_rows, KV, 2, HD)
    keys = keyval_all[:, :, 0]
    values = keyval_all[:, :, 1]
    row_order = jnp.arange(group_rows)
    allowed = (segments[:, None] == segments[None, :]) & (row_order[None, :] <= row_order[:, None])
    softmax_rows, softmax_low, attended = attend(queries, keys, values, allowed)

    next_row = (pipe_rank + 1) * block_rows
    att_turned = jnp.roll(attended.reshape(group_rows, head_cols), -next_row, axis=0)
    att_turned = att_turned.reshape(pipe_count, block_rows, head_cols)
    mine = [att_turned[0]] + [
        by_shift(att_turned[pipe_count - m], -m, "pipe") for m in range(1, pipe_count)
    ]
    att_found = gather_peers(jnp.concatenate(mine, axis=1), "dp")
    att_rows = jnp.concatenate([att_found[peer] for peer in order], axis=0)
    partial_out = jnp.dot(att_rows, out_weights, preferred_element_type=wide)
    shallow_block = lax.dynamic_slice_in_dim(
        columns.reshape(data_count, group_rows, slice_cols),
        next_row % group_rows,
        block_rows,
        1,
    )
    output = (partial_out + shallow_block.reshape(-1, slice_cols).astype(wide))
    sums = jnp.stack(
        [
            jnp.sum(output * output, axis=-1),
            jnp.sum(target * target, axis=-1),
            jnp.sum(output * target, axis=-1),
        ],
        axis=-1,
    )
    sums = sum_peer_rows(sums.reshape(data_count, block_rows * 3), "dp")
    sums = sums.reshape(data_count * block_rows, 3)
    norm_out = jnp.sqrt(sums[:, 0:1] + cosine_eps)
    norm_tar = jnp.sqrt(sums[:, 1:2] + cosine_eps)
    cosine_sim = sums[:, 2:3] / (norm_out * norm_tar)
    loss_local = jnp.sum(1.0 - cosine_sim[:block_rows])
    out_grad = (
        -(target / (norm_out * norm_tar) - cosine_sim * output / (norm_out * norm_out)) / all_rows
    ).astype(low)

    block_half = half_count * block_rows
    width = out_weights.shape[0]
    grad_send = contract_cols(out_grad[block_half:], out_weights).astype(low)
    grad_keep = contract_cols(out_grad[:block_half], out_weights)
    att_block = reduce_peers(
        grad_keep.reshape(half_count, block_rows, width),
        grad_send.reshape(half_count, block_rows, width),
        "dp",
    )
    att_block = att_block.astype(low).reshape(block_rows, pipe_count, head_cols)
    back = [att_block[:, 0]] + [by_shift(att_block[:, m], m, "pipe") for m in range(1, pipe_count)]
    back = jnp.concatenate([back[(-m) % pipe_count] for m in range(pipe_count)], axis=0)
    att_grad = jnp.roll(back, next_row, axis=0).reshape(group_rows, local_heads // KV, KV, HD)

    out_grads = jnp.stack(
        [g.reshape(data_count, block_rows, slice_cols) for g in gather_line(out_grad, "pipe")],
        axis=1,
    )
    turned, _ = lax.optimization_barrier((att_turned.reshape(group_rows, head_cols), att_block))
    turned_found = gather_peers(turned, "dp")
    turned_all = jnp.concatenate([turned_found[peer] for peer in order], axis=0)
    grad_output = contract_rows(turned_all, out_grads.reshape(all_rows, slice_cols))

    query_part, key_part, value_part = attend_grad(
        softmax_rows, softmax_low, queries, keys, values, att_grad
    )
    query_grad = unrotate(
        query_part.reshape(group_rows, local_heads, HD), cosine, sine_table
    ).reshape(group_rows, head_cols)
    query_grad = (query_grad * row_scale).astype(low)
    keyval_part = jnp.stack([key_part, value_part], axis=2).astype(low)
    keyval_part = keyval_part.reshape(group_rows, pipe_count, keyval_cols).transpose(1, 0, 2)
    keyval_part = jnp.roll(keyval_part, -pipe_rank, axis=0)
    keyval_sum = keyval_part[0].astype(wide)
    for m in range(1, pipe_count):
        keyval_sum = keyval_sum + by_shift(keyval_part[m], m, "pipe").astype(wide)
    keyval_sum = keyval_sum.reshape(group_rows, keyval_blocks, HD)
    keyval_grad = jnp.where(is_key, unrotate(keyval_sum, cosine, sine_table), keyval_sum)
    keyval_grad = (keyval_grad.reshape(group_rows, keyval_cols) * row_scale).astype(low)
    query_found = gather_peers(query_grad, "dp")
    keyval_found = gather_peers(keyval_grad, "dp")
    query_all = jnp.concatenate([query_found[peer] for peer in order], axis=0)
    keyval_all_grad = jnp.concatenate([keyval_found[peer] for peer in order], axis=0)
    grad_query = contract_rows(columns, query_all) * gain
    grad_keyval = contract_rows(columns, keyval_all_grad) * gain
    squares = (
        jnp.sum(grad_query * grad_query)
        + jnp.sum(grad_keyval * grad_keyval)
        + jnp.sum(grad_output * grad_output)
    )
    totals = jnp.stack([squares, loss_local])
    totals = sum_peers(sum_peers(totals, "dp"), "pipe")
    grad_rms = jnp.sqrt(totals[0] / param_count + mean_eps)
    return (
        totals[1] / all_rows,
        grad_query / grad_rms,
        grad_keyval / grad_rms,
        grad_output / grad_rms,
    )


def solution(mesh):
    placed = (
        P("dp", None),
        P(("dp", "pipe"), None),
        P("dp"),
        P("dp"),
        P(),
        P("dp", "pipe"),
        P("dp", "pipe"),
        P("pipe", "dp"),
    )
    return jax.shard_map(
        per_device,
        mesh=mesh,
        in_specs=placed,
        out_specs=(P(), P("dp", "pipe"), P("dp", "pipe"), P("pipe", "dp")),
        check_vma=False,
    )
```
